512 devices in a mesh: ctx: 64 (over x, y, core), tp: 8 (over z).
Axes of the slice: x: 4, y: 8, z: 8, core: 2. Of those that a mesh axis runs over, the one named last changes fastest.
Arguments:
- q_one: bfloat16 [16384, 8192], P('ctx', 'tp'), may hold values from -6 to 6
- k_one: bfloat16 [16384, 8192], P('ctx', 'tp'), may hold values from -40 to 40, as said below
- v_one: bfloat16 [16384, 8192], P('ctx', 'tp'), may hold values from -6 to 6
- mr_filter: bfloat16 [512, 128], P('tp'), may hold values from -3.535534 to 3.535534
- norm_gain: float32 [8192], P('tp'), may hold values from 0.1 to 1.9
- q_two: bfloat16 [16384, 8192], P('ctx', 'tp'), may hold values from -6 to 6
- k_two: bfloat16 [16384, 8192], P('ctx', 'tp'), may hold values from -6 to 6
- li_rates: float32 [16, 8192], P(None, 'tp'), may hold values from 1.5258789e-05 to 0.03
- li_residues: float32 [16, 8192], P(None, 'tp'), may hold values from -4 to 4
Outputs:
- mixed: bfloat16 [16384, 8192], P('ctx', 'tp')
The draws below stay inside these ranges and needn't reach their ends.
Inputs may be any that keep to these rules, and one draw needn't show every extreme that they name: Each row of k_one has a scale of its own.
All inputs are finite; a program needn't handle non-finite values.
Results may differ from the reference program's by a relative error of at most 0.0057.
Values may be sent and summed in bfloat16 or wider, within the bound.
No kernel may reach another device: no remote copies, remote signals or barrier semaphores. Data moves between devices by JAX's collectives and lax.ppermute only.
A program may use at most 128 MiB of HBM per device.

```python
import math
import jax
import jax.numpy as jnp
from jax import lax

D = 8192
TOK_DEV = 256
KMR = 128
MODES = 16
MR_GROUP = 16
SEQ = 16384
MR_FILTERS = 512


def draw_k_one(key, part):
    base_key = jax.random.fold_in(key, 11)
    scale_key = jax.random.fold_in(key, 12)
    base = jnp.clip(jax.random.normal(base_key, (SEQ, D), jnp.float32), -4.0, 4.0)
    row_scale = 10.0 ** jax.random.uniform(scale_key, (SEQ, 1), jnp.float32, 0.0, 1.0)
    return (base * row_scale).astype(jnp.bfloat16)


def draw_mr_filter(key, part):
    base_key = jax.random.fold_in(key, 21)
    base = jnp.clip(jax.random.normal(base_key, (MR_FILTERS, KMR), jnp.float32), -4.0, 4.0)
    ramp = jnp.arange(MR_FILTERS).astype(jnp.float32) / MR_FILTERS
    scaled = base * (10.0 ** ramp)[:, None] / KMR ** 0.5
    return scaled.astype(jnp.bfloat16)


def level_of(key, extent, cuts, smallest, top_value):
    level = 1.0
    for dim, blocks in cuts:
        steps = jax.random.uniform(jax.random.fold_in(jax.random.fold_in(key, 6), dim), (blocks,), jnp.float32, smallest / len(cuts), top_value / len(cuts))
        level = level * jnp.repeat(jnp.exp(steps), extent[dim] // blocks).reshape((-1,) + (1,) * (len(extent) - 1 - dim))
    return level


def scatter_about(own_key, dims, deviation, most, shards=(), kind=jnp.bfloat16):
    values = jax.random.normal(own_key, dims, jnp.float32) * deviation
    if len(shards) > 0:
        values = level_of(own_key, dims, shards, -0.22, 0.18) * values
    return jnp.clip(values, min=-most, max=most).astype(kind)


def setup_inputs(seed: int = 0) -> dict:
    seeds = jax.random.split(jax.random.key(seed), 10)
    return {
        "q_one": scatter_about(seeds[0], (SEQ, D), 1.0, 6.0, ((0, 64), (1, 8))),
        "k_one": draw_k_one(jax.random.fold_in(seeds[9], 71), 0),
        "v_one": scatter_about(seeds[2], (SEQ, D), 1.0, 6.0, ((0, 64), (1, 8))),
        "mr_filter": draw_mr_filter(jax.random.fold_in(seeds[9], 71), 0),
        "norm_gain": jnp.clip(1.0 + 0.18 * jax.random.normal(seeds[4], (D,), jnp.float32), 0.1, 1.9),
        "q_two": scatter_about(seeds[5], (SEQ, D), 1.0, 6.0, ((0, 64), (1, 8))),
        "k_two": scatter_about(seeds[6], (SEQ, D), 1.0, 6.0, ((0, 64), (1, 8))),
        "li_rates": jnp.clip(jnp.exp(math.log(0.03) - 7.583797 * jax.random.uniform(seeds[7], (MODES, D), jnp.float32) ** level_of(seeds[7], (MODES, D), ((1, 8),), -0.2, 0.2)), 1.52587890625e-05, 0.03),
        "li_residues": scatter_about(seeds[8], (MODES, D), 0.25, 4.0, ((1, 8),), jnp.float32),
    }


def join_states(earlier, later):
    return (earlier[0] * later[0], later[0] * earlier[1] + later[1])

def modal_parts(rates, residues, sub_len):
    norm_scale = jnp.sqrt(-jnp.expm1(-2.0 * rates))
    weights = residues * norm_scale
    lags = jnp.arange(sub_len).astype(jnp.float32)
    powers = jnp.exp(-rates[:, None, :] * lags[None, :, None])
    kernel = lax.optimization_barrier(jnp.sum(weights[:, None, :] * powers, axis=0))
    lag_table = jnp.arange(sub_len)[:, None] - jnp.arange(sub_len)[None, :]
    toeplitz = jnp.where((lag_table >= 0)[:, :, None], kernel[jnp.clip(lag_table, 0, sub_len - 1)], 0.0)
    closing_w = powers[:, ::-1, :]
    entry_w = weights[:, None, :] * powers * jnp.exp(-rates)[:, None, :]
    stride_decay = jnp.exp(-rates * sub_len)
    return (toeplitz, closing_w, entry_w, stride_decay)

def local_pass(signal, parts):
    toeplitz, closing_w, entry_w, stride_decay = parts
    inner = jnp.einsum('ijc,bjc->bic', toeplitz, signal, precision=lax.Precision.HIGHEST)
    closing = jnp.einsum('mjc,bjc->bmc', closing_w, signal, precision=lax.Precision.HIGHEST)
    decays = jnp.broadcast_to(stride_decay, closing.shape)
    _, states = lax.associative_scan(join_states, (decays, closing), axis=0)
    return (inner, states)

def finish(inner, states, incoming, rates, parts):
    entry_w = parts[2]
    sub_len = inner.shape[1]
    prior = jnp.concatenate([jnp.zeros_like(states[:1]), states[:-1]], axis=0)
    count = jnp.arange(inner.shape[0]).astype(jnp.float32)[:, None, None]
    prior = prior + jnp.exp(-rates[None] * (sub_len * count)) * incoming[None]
    return inner + jnp.einsum('mic,bmc->bic', entry_w, prior, precision=lax.Precision.HIGHEST)

def reference(q_one, k_one, v_one, mr_filter, norm_gain, q_two, k_two, li_rates, li_residues):
    u_one = (k_one.astype(jnp.float32) * v_one.astype(jnp.float32)).astype(jnp.bfloat16)
    taps = mr_filter.shape[1]
    chan_taps = jnp.repeat(mr_filter.astype(jnp.float32), MR_GROUP, axis=0).T
    padded = jnp.concatenate([jnp.zeros((taps - 1, D), jnp.float32), u_one.astype(jnp.float32)], axis=0)

    def add_tap(index, total):
        piece = lax.dynamic_slice_in_dim(padded, taps - 1 - index, SEQ, 0)
        return total + piece * lax.dynamic_index_in_dim(chan_taps, index, 0, keepdims=False)[None, :]
    conv_one = lax.fori_loop(0, taps, add_tap, jnp.zeros((SEQ, D), jnp.float32))
    z_one = q_one.astype(jnp.float32) * conv_one
    squares = lax.optimization_barrier(jnp.sum(z_one * z_one, axis=1))
    scaled = z_one * lax.rsqrt(squares / D + 1e-06)[:, None] * norm_gain[None, :]
    u_two = (k_two.astype(jnp.float32) * scaled).astype(jnp.bfloat16)
    sub_len = min(32, TOK_DEV)
    parts = modal_parts(li_rates, li_residues, sub_len)
    signal = u_two.astype(jnp.float32).reshape(SEQ // sub_len, sub_len, D)
    inner, states = local_pass(signal, parts)
    conv_two = finish(inner, states, jnp.zeros((MODES, D), jnp.float32), li_rates, parts).reshape(SEQ, D)
    return (q_two.astype(jnp.float32) * conv_two).astype(jnp.bfloat16)
```

```python
import functools

import jax
import jax.numpy as jnp
from jax import lax
from jax.experimental import pallas as pl
from jax.experimental.pallas import tpu as pltpu
from jax.sharding import PartitionSpec as P

LANES = 128
ROWS = 8
UNROLL = 8
F32 = jnp.float32
BF16 = jnp.bfloat16
INTERPRET = False


def in_vmem(count):
    return [pl.BlockSpec(memory_space=pltpu.VMEM)] * count


def call(kernel, out_shape, args, scratch=(), smem=0, name=None):
    specs = [pl.BlockSpec(memory_space=pltpu.SMEM)] * smem + in_vmem(len(args) - smem)
    outs = in_vmem(len(out_shape)) if isinstance(out_shape, (list, tuple)) else in_vmem(1)[0]
    return pl.pallas_call(
        kernel,
        out_shape=out_shape,
        in_specs=specs,
        out_specs=outs,
        scratch_shapes=list(scratch),
        name=name,
        interpret=INTERPRET,
    )(*args)


def shape(dims, kind=F32):
    return jax.ShapeDtypeStruct(dims, kind)


def channel_rows(ref, table):
    modes = table.shape[0]
    for block in range(table.shape[1] // LANES):
        piece = table[:, block * LANES : (block + 1) * LANES]
        ref[pl.ds(block, modes, stride=ROWS), :] = piece


def tables_kernel(span, filter_ref, rates_ref, weights_ref, tap_ref, step_ref, weight_ref, decay_ref):
    groups, taps = filter_ref.shape
    row = lax.broadcasted_iota(jnp.int32, (taps, taps), 0)
    col = lax.broadcasted_iota(jnp.int32, (taps, taps), 1)
    flip = jnp.where(((row + col) & (taps - 1)) == 0, 1.0, 0.0).astype(BF16)
    mirrored = jnp.dot(filter_ref[...], flip, preferred_element_type=F32)
    before = col > row
    for group in range(groups):
        line = jnp.broadcast_to(mirrored[group : group + 1, :], (taps, taps))
        circulant = pltpu.roll(line, 0, axis=1, stride=1, stride_axis=0)
        tap_ref[group, :, :taps] = jnp.where(before, circulant, 0.0).astype(BF16)
        tap_ref[group, :, taps:] = jnp.where(before, 0.0, circulant).astype(BF16)
    rates = rates_ref[...]
    channel_rows(step_ref, jnp.exp(-rates))
    channel_rows(decay_ref, jnp.exp(-rates * span))
    channel_rows(weight_ref, weights_ref[...])


def conv_kernel(
    group_ch, k_ref, v_ref, q_ref, gate_ref, gain_ref, halo_ref, tap_ref, value_ref, square_ref
):
    length, channels = k_ref.shape
    half = length // 2
    lane = lax.broadcasted_iota(jnp.int32, (half, 2 * LANES), 1)
    member = (lane & (LANES - 1)) // group_ch
    per_tile = LANES // group_ch
    partial = [jnp.zeros((half, LANES), F32), jnp.zeros((half, LANES), F32)]
    for tile in range(channels // LANES):
        cols = slice(tile * LANES, (tile + 1) * LANES)
        u_one = (k_ref[:, cols].astype(F32) * v_ref[:, cols].astype(F32)).astype(BF16)
        early = jnp.concatenate([halo_ref[:, cols], u_one[:half]], axis=0)
        windows = jnp.concatenate([early, u_one], axis=1)
        conv = jnp.zeros((half, 2 * LANES), F32)
        for place in range(per_tile):
            product = jnp.dot(
                tap_ref[tile * per_tile + place], windows, preferred_element_type=F32
            )
            conv = jnp.where(member == place, product, conv)
        for part in range(2):
            rows = slice(part * half, (part + 1) * half)
            z_one = q_ref[rows, cols].astype(F32) * conv[:, part * LANES : (part + 1) * LANES]
            partial[part] = partial[part] + z_one * z_one
            value = gate_ref[rows, cols].astype(F32) * (z_one * gain_ref[:, cols])
            value_ref[pl.ds(part * half * ROWS + tile, half, stride=ROWS), :] = value
    for part in range(2):
        line = jnp.sum(partial[part].T, axis=0, keepdims=True)
        for copy in range(square_ref.shape[0]):
            square_ref[copy, part : part + 1, :] = line


def state_kernel(width, square_ref, value_ref, step_ref, u_ref, state_ref, scale_ref):
    half = LANES
    total = square_ref[0]
    for peer in range(1, square_ref.shape[0]):
        total = total + square_ref[peer]
    scale = lax.rsqrt(total / width + 1e-06)
    for part in range(2):
        line = jnp.broadcast_to(scale[part : part + 1, :], (half, LANES))
        scale_ref[part * half : (part + 1) * half, :] = line.T
    modes = step_ref.shape[0] // ROWS
    steps = [step_ref[m * ROWS : (m + 1) * ROWS, :] for m in range(modes)]

    def token(t, states):
        at = pl.ds(pl.multiple_of(t * ROWS, ROWS), ROWS)
        factor = jnp.broadcast_to(scale_ref[pl.ds(t, 1), :], (ROWS, LANES))
        u_two = (value_ref[at, :] * factor).astype(BF16).astype(F32)
        u_ref[at, :] = u_two
        return tuple(a * s + u_two for a, s in zip(steps, states))

    zero = tuple(jnp.zeros((ROWS, LANES), F32) for _ in range(modes))
    states = lax.fori_loop(0, 2 * half, token, zero, unroll=UNROLL)
    for m in range(modes):
        state_ref[m * ROWS : (m + 1) * ROWS, :] = states[m]


def scan_kernel(place_ref, state_ref, decay_ref, entry_ref):
    decay = decay_ref[place_ref[0]]
    entry = jnp.zeros_like(decay)
    for device in range(state_ref.shape[0]):
        entry_ref[device] = entry
        entry = decay * entry + state_ref[device]


def output_kernel(entry_ref, u_ref, step_ref, weight_ref, gate_ref, out_ref, conv_ref):
    modes = step_ref.shape[0] // ROWS
    rows_of = lambda ref: [ref[m * ROWS : (m + 1) * ROWS, :] for m in range(modes)]
    steps, weights = rows_of(step_ref), rows_of(weight_ref)
    length, channels = gate_ref.shape

    def token(t, states):
        at = pl.ds(pl.multiple_of(t * ROWS, ROWS), ROWS)
        u_two = u_ref[at, :]
        states = tuple(a * s + u_two for a, s in zip(steps, states))
        terms = [w * s for w, s in zip(weights, states)]
        while len(terms) > 1:
            terms = [x + y for x, y in zip(terms[::2], terms[1::2])]
        conv_ref[at, :] = terms[0]
        return states

    lax.fori_loop(0, length, token, tuple(rows_of(entry_ref)), unroll=UNROLL)
    for tile in range(channels // LANES):
        cols = slice(tile * LANES, (tile + 1) * LANES)
        conv_two = conv_ref[pl.ds(tile, length, stride=ROWS), :]
        out_ref[:, cols] = (gate_ref[:, cols].astype(F32) * conv_two).astype(BF16)


def on_device(q_one, k_one, v_one, mr_filter, norm_gain, q_two, k_two, li_rates, li_residues):
    length, channels = q_one.shape
    groups, taps = mr_filter.shape
    modes = li_rates.shape[0]
    devices, peers = lax.axis_size("ctx"), lax.axis_size("tp")
    width = channels * peers
    flat = (modes * ROWS, LANES)

    tail = (k_one[length - taps :].astype(F32) * v_one[length - taps :].astype(F32)).astype(BF16)
    halo = lax.ppermute(tail, "ctx", [(i, i + 1) for i in range(devices - 1)])

    weights = li_residues * jnp.sqrt(-jnp.expm1(-2.0 * li_rates))
    tap_table, steps, mode_weights, decays = call(
        functools.partial(tables_kernel, float(length)),
        [shape((groups, taps, 2 * taps), BF16), shape(flat), shape(flat), shape(flat)],
        (mr_filter, li_rates, weights),
        name="tables",
    )
    value, squares = call(
        functools.partial(conv_kernel, channels // groups),
        [shape((length * ROWS, LANES)), shape((peers, 2, LANES))],
        (k_one, v_one, q_one, k_two, norm_gain[None, :], halo, tap_table),
        name="conv",
    )
    squares = lax.all_to_all(squares, "tp", split_axis=0, concat_axis=0, tiled=True)
    u_two, states = call(
        functools.partial(state_kernel, float(width)),
        [shape((length * ROWS, LANES)), shape(flat)],
        (squares, value, steps),
        scratch=[pltpu.VMEM((length, LANES), F32)],
        name="states",
    )
    shares = (devices, flat[0] // devices, LANES)
    received = lax.all_to_all(
        states.reshape(shares), "ctx", split_axis=0, concat_axis=0, tiled=True
    )
    place = lax.axis_index("ctx").astype(jnp.int32).reshape(1)
    entries = call(
        scan_kernel,
        shape(shares),
        (place, received, decays.reshape(shares)),
        smem=1,
        name="scan",
    )
    entries = lax.all_to_all(entries, "ctx", split_axis=0, concat_axis=0, tiled=True)
    return call(
        output_kernel,
        shape((length, channels), BF16),
        (entries.reshape(flat), u_two, steps, mode_weights, q_two),
        scratch=[pltpu.VMEM((length * ROWS, LANES), F32)],
        name="output",
    )


def solution(mesh):
    in_specs = (
        P("ctx", "tp"),
        P("ctx", "tp"),
        P("ctx", "tp"),
        P("tp", None),
        P("tp"),
        P("ctx", "tp"),
        P("ctx", "tp"),
        P(None, "tp"),
        P(None, "tp"),
    )
    return jax.shard_map(
        on_device, mesh=mesh, in_specs=in_specs, out_specs=P("ctx", "tp"), check_vma=False
    )
```

```python
import functools

import jax
import jax.numpy as jnp
from jax import lax
from jax.experimental import pallas as pl
from jax.experimental.pallas import tpu as pltpu
from jax.sharding import PartitionSpec as P

LANES = 128
ROWS = 8
BLOCK = 64
UNROLL = 8
CHUNK = 16
QUARTERS = 4
F32 = jnp.float32
BF16 = jnp.bfloat16
INTERPRET = False
IN_VMEM = pl.BlockSpec(memory_space=pltpu.VMEM)
IN_SMEM = pl.BlockSpec(memory_space=pltpu.SMEM)
IN_HBM = pl.BlockSpec(memory_space=pltpu.HBM)


def hbm(array):
    return array if INTERPRET else pltpu.with_memory_space_constraint(array, pltpu.HBM)


def call(name, kernel, inputs, outputs, scratch=()):
    return pl.pallas_call(
        kernel,
        out_shape=[jax.ShapeDtypeStruct(dims, kind) for _, dims, kind in outputs],
        in_specs=[spec for spec, _ in inputs],
        out_specs=[spec for spec, _, _ in outputs],
        scratch_shapes=list(scratch),
        compiler_params=pltpu.CompilerParams(vmem_limit_bytes=16 * 2**20),
        interpret=INTERPRET,
        name=name,
    )(*[hbm(array) if spec is IN_HBM else array for spec, array in inputs])


def fetch(pairs, sems):
    copies = [
        pltpu.make_async_copy(source, target, sems.at[i])
        for i, (source, target) in enumerate(pairs)
    ]
    for copy in copies:
        copy.start()
    return copies


def channel_rows(ref, table):
    modes = table.shape[0]
    for block in range(table.shape[1] // LANES):
        piece = table[:, block * LANES : (block + 1) * LANES]
        ref[pl.ds(block, modes, stride=ROWS), :] = piece


def one_minus_exp(x):
    total = jnp.full_like(x, 1.0)
    for order in range(11, 1, -1):
        total = 1.0 - total * x * (1.0 / order)
    return jnp.where(x < 0.5, x * total, 1.0 - jnp.exp(-x))


def product_bf16(left, right):
    return (left.astype(F32) * right.astype(F32)).astype(BF16)


def filtered(tap_ref, tile, per_tile, windows, member):
    conv = None
    for place in range(per_tile):
        product = jnp.dot(tap_ref[tile * per_tile + place], windows, preferred_element_type=F32)
        conv = product if place == 0 else jnp.where(member == place, product, conv)
    return conv


def gated(conv, tile, q, gate, gain, partial, value_ref):
    for part in range(2):
        rows = slice(part * BLOCK, (part + 1) * BLOCK)
        z_one = q[rows].astype(F32) * conv[:, part * LANES : (part + 1) * LANES]
        partial[part] = partial[part] + z_one * z_one
        value = gate[rows].astype(F32) * (z_one * gain)
        value_ref[pl.ds(part * BLOCK * ROWS + tile, BLOCK, stride=ROWS), :] = value


def token_row(partial):
    return jnp.sum(jnp.concatenate(partial, axis=0).T, axis=0, keepdims=True)


def lane_member(group_ch):
    lane = lax.broadcasted_iota(jnp.int32, (BLOCK, 2 * LANES), 1)
    return (lane & (LANES - 1)) // group_ch


def tail_kernel(k_hbm, v_hbm, tail_ref, k_ref, v_ref, sems):
    rows = pl.ds(k_hbm.shape[0] - tail_ref.shape[0], tail_ref.shape[0])
    for copy in fetch([(k_hbm.at[rows, :], k_ref), (v_hbm.at[rows, :], v_ref)], sems):
        copy.wait()
    tail_ref[...] = product_bf16(k_ref[...], v_ref[...])


def late_kernel(
    group_ch,
    k_hbm,
    v_hbm,
    q_hbm,
    gate_hbm,
    filter_hbm,
    gain_hbm,
    rates_hbm,
    tap_ref,
    u_ref,
    q_early_ref,
    gate_early_ref,
    gain_ref,
    step_ref,
    value_ref,
    square_ref,
    k_ref,
    v_ref,
    q_ref,
    gate_ref,
    filter_ref,
    rates_ref,
    sems,
):
    length, channels = k_hbm.shape
    half = length // 2
    early, late = pl.ds(0, half), pl.ds(half, half)
    copies = fetch(
        [
            (filter_hbm, filter_ref),
            (k_hbm, k_ref),
            (v_hbm, v_ref),
            (q_hbm.at[late, :], q_ref),
            (gate_hbm.at[late, :], gate_ref),
            (gain_hbm, gain_ref),
            (rates_hbm, rates_ref),
            (q_hbm.at[early, :], q_early_ref),
            (gate_hbm.at[early, :], gate_early_ref),
        ],
        sems,
    )
    copies[0].wait()
    groups, taps = filter_ref.shape
    row = lax.broadcasted_iota(jnp.int32, (taps, taps), 0)
    col = lax.broadcasted_iota(jnp.int32, (taps, taps), 1)
    flip = jnp.where(((row + col) & (taps - 1)) == 0, 1.0, 0.0).astype(BF16)
    mirrored = jnp.dot(filter_ref[...], flip, preferred_element_type=F32)
    before = (col > row)[:BLOCK]
    for group in range(groups):
        line = jnp.broadcast_to(mirrored[group : group + 1, :], (BLOCK, taps))
        circulant = pltpu.roll(line, 0, axis=1, stride=1, stride_axis=0)
        tap_ref[group, :, :taps] = jnp.where(before, circulant, 0.0).astype(BF16)
        tap_ref[group, :, taps:] = jnp.where(before, 0.0, circulant).astype(BF16)
    for copy in copies[1:7]:
        copy.wait()
    channel_rows(step_ref, jnp.exp(-rates_ref[...]))
    member = lane_member(group_ch)
    partial = [jnp.zeros((BLOCK, LANES), F32) for _ in range(2)]
    none = jnp.zeros((BLOCK, LANES), BF16)
    for tile in range(channels // LANES):
        cols = slice(tile * LANES, (tile + 1) * LANES)
        u_one = product_bf16(k_ref[:, cols], v_ref[:, cols])
        u_ref[:, cols] = u_one[:half]
        later = jnp.concatenate([u_one[BLOCK:], none], axis=0)
        windows = jnp.concatenate([u_one, later], axis=1)
        conv = filtered(tap_ref, tile, LANES // group_ch, windows, member)
        gated(conv, tile, q_ref[:, cols], gate_ref[:, cols], gain_ref[:, cols], partial, value_ref)
    square_ref[...] = token_row(partial)
    for copy in copies[7:]:
        copy.wait()


def early_kernel(
    group_ch,
    halo_ref,
    tap_ref,
    u_ref,
    q_ref,
    gate_ref,
    gain_ref,
    late_ref,
    value_ref,
    square_ref,
):
    member = lane_member(group_ch)
    partial = [jnp.zeros((BLOCK, LANES), F32) for _ in range(2)]
    none = jnp.zeros((BLOCK, LANES), BF16)
    for tile in range(u_ref.shape[1] // LANES):
        cols = slice(tile * LANES, (tile + 1) * LANES)
        halo, u_one = halo_ref[:, cols], u_ref[:, cols]
        first = jnp.concatenate([halo, u_one], axis=0)
        second = jnp.concatenate([halo[BLOCK:], u_one, none], axis=0)
        windows = jnp.concatenate([first, second], axis=1)
        conv = filtered(tap_ref, tile, LANES // group_ch, windows, member)
        gated(conv, tile, q_ref[:, cols], gate_ref[:, cols], gain_ref[:, cols], partial, value_ref)
    line = token_row(partial)
    for copy in range(square_ref.shape[0]):
        square_ref[copy, 0:1, :] = line
        square_ref[copy, 1:2, :] = late_ref[...]


def mode_rows(ref):
    return [ref[at : at + ROWS, :] for at in range(0, ref.shape[0], ROWS)]


def token_rows(t):
    return pl.ds(pl.multiple_of(t * ROWS, ROWS), ROWS)


def tree_sum(terms):
    while len(terms) > 1:
        terms = [x + y for x, y in zip(terms[::2], terms[1::2])]
    return terms[0]


def state_kernel(width, square_ref, early_ref, late_ref, step_ref, u_ref, state_ref, scale_ref):
    total = square_ref[0]
    for peer in range(1, square_ref.shape[0]):
        total = total + square_ref[peer]
    scale = lax.rsqrt(total / width + 1e-06)
    for part in range(2):
        line = jnp.broadcast_to(scale[part : part + 1, :], (LANES, LANES))
        scale_ref[part * LANES : (part + 1) * LANES, :] = line.T
    steps = mode_rows(step_ref)
    states = tuple(jnp.zeros((ROWS, LANES), F32) for _ in steps)
    for part, value_ref in enumerate((early_ref, late_ref)):

        def token(t, states):
            place = t + part * LANES
            factor = jnp.broadcast_to(scale_ref[pl.ds(place, 1), :], (ROWS, LANES))
            u_two = (value_ref[token_rows(t), :] * factor).astype(BF16).astype(F32)
            u_ref[token_rows(place), :] = u_two
            return tuple(a * s + u_two for a, s in zip(steps, states))

        states = lax.fori_loop(0, LANES, token, states, unroll=UNROLL)
    for m, state in enumerate(states):
        state_ref[m * ROWS : (m + 1) * ROWS, :] = state


def inner_kernel(
    share,
    place_ref,
    u_ref,
    step_ref,
    rates_hbm,
    residues_hbm,
    conv_ref,
    weight_ref,
    decay_ref,
    rates_ref,
    residues_ref,
    decays_ref,
    sems,
):
    for copy in fetch([(rates_hbm, rates_ref), (residues_hbm, residues_ref)], sems):
        copy.wait()
    rates = rates_ref[...]
    tokens = u_ref.shape[0] // ROWS
    channel_rows(decays_ref, jnp.exp(-rates * float(tokens)))
    decay_ref[...] = decays_ref[pl.ds(place_ref[0] * share, share), :]
    channel_rows(weight_ref, residues_ref[...] * jnp.sqrt(one_minus_exp(2.0 * rates)))
    steps, weights = mode_rows(step_ref), mode_rows(weight_ref)

    def token(t, states):
        u_two = u_ref[token_rows(t), :]
        states = tuple(a * s + u_two for a, s in zip(steps, states))
        conv_ref[token_rows(t), :] = tree_sum([w * s for w, s in zip(weights, states)])
        return states

    zero = tuple(jnp.zeros((ROWS, LANES), F32) for _ in steps)
    lax.fori_loop(0, tokens, token, zero, unroll=UNROLL)


def scan_kernel(state_ref, decay_ref, entry_ref):
    decay = decay_ref[...]
    entry = jnp.zeros_like(decay)
    for device in range(state_ref.shape[0]):
        entry_ref[device] = entry
        entry = decay * entry + state_ref[device]


def output_kernel(
    entry_ref, conv_ref, step_ref, weight_ref, gate_ref, out_hbm, sum_ref, out_ref, sems
):
    steps = mode_rows(step_ref)
    carried = tuple(w * e for w, e in zip(mode_rows(weight_ref), mode_rows(entry_ref)))
    length, channels = gate_ref.shape

    def advance(chunk, carried):
        for t in range(CHUNK):
            carried = tuple(a * e for a, e in zip(steps, carried))
            at = token_rows(chunk * CHUNK + t)
            sum_ref[at, :] = conv_ref[at, :] + tree_sum(list(carried))
        return carried

    def emit(chunk):
        rows = pl.ds(pl.multiple_of(chunk * CHUNK, CHUNK), CHUNK)
        for tile in range(channels // LANES):
            cols = slice(tile * LANES, (tile + 1) * LANES)
            conv_two = sum_ref[pl.ds(chunk * (CHUNK * ROWS) + tile, CHUNK, stride=ROWS), :]
            out_ref[rows, cols] = (gate_ref[rows, cols].astype(F32) * conv_two).astype(BF16)

    def both(chunk, carried):
        emit(chunk - 1)
        return advance(chunk, carried)

    chunks = length // CHUNK
    per_quarter = chunks // QUARTERS
    copies = []
    carried = advance(0, carried)
    for quarter in range(QUARTERS):
        last = (quarter + 1) * per_quarter
        first = quarter * per_quarter + 1
        carried = lax.fori_loop(first, min(last + 1, chunks), both, carried)
        if last == chunks:
            emit(chunks - 1)
        rows = pl.ds(quarter * per_quarter * CHUNK, per_quarter * CHUNK)
        copy = pltpu.make_async_copy(out_ref.at[rows, :], out_hbm.at[rows, :], sems.at[quarter])
        copy.start()
        copies.append(copy)
    for copy in copies:
        copy.wait()


def on_device(q_one, k_one, v_one, mr_filter, norm_gain, q_two, k_two, li_rates, li_residues):
    length, channels = q_one.shape
    groups, taps = mr_filter.shape
    modes = li_rates.shape[0]
    devices, peers = lax.axis_size("ctx"), lax.axis_size("tp")
    group_ch = channels // groups
    half = length // 2
    flat = (modes * ROWS, LANES)
    shares = (devices, flat[0] // devices, LANES)
    place = lax.axis_index("ctx").astype(jnp.int32).reshape(1)

    (tail,) = call(
        "tail",
        tail_kernel,
        [(IN_HBM, k_one), (IN_HBM, v_one)],
        [(IN_VMEM, (taps, channels), BF16)],
        [pltpu.VMEM((taps, channels), BF16)] * 2 + [pltpu.SemaphoreType.DMA((2,))],
    )
    halo = lax.ppermute(tail, "ctx", [(i, i + 1) for i in range(devices - 1)])
    late = call(
        "late",
        functools.partial(late_kernel, group_ch),
        [
            (IN_HBM, k_one),
            (IN_HBM, v_one),
            (IN_HBM, q_one),
            (IN_HBM, k_two),
            (IN_HBM, mr_filter),
            (IN_HBM, norm_gain[None, :]),
            (IN_HBM, li_rates),
        ],
        [
            (IN_VMEM, (groups, BLOCK, 2 * taps), BF16),
            (IN_VMEM, (half, channels), BF16),
            (IN_VMEM, (half, channels), BF16),
            (IN_VMEM, (half, channels), BF16),
            (IN_VMEM, (1, channels), F32),
            (IN_VMEM, flat, F32),
            (IN_VMEM, (half * ROWS, LANES), F32),
            (IN_VMEM, (1, half), F32),
        ],
        [
            pltpu.VMEM((length, channels), BF16),
            pltpu.VMEM((length, channels), BF16),
            pltpu.VMEM((half, channels), BF16),
            pltpu.VMEM((half, channels), BF16),
            pltpu.VMEM((groups, taps), BF16),
            pltpu.VMEM((modes, channels), F32),
            pltpu.SemaphoreType.DMA((9,)),
        ],
    )
    tap_table, u_early, q_early, gate_early, gain, steps, value_late, square_late = late
    value_early, squares = call(
        "early",
        functools.partial(early_kernel, group_ch),
        [
            (IN_VMEM, array)
            for array in (halo, tap_table, u_early, q_early, gate_early, gain, square_late)
        ],
        [(IN_VMEM, (half * ROWS, LANES), F32), (IN_VMEM, (peers, 2, LANES), F32)],
    )
    squares = lax.all_to_all(squares, "tp", split_axis=0, concat_axis=0, tiled=True)
    u_two, states = call(
        "states",
        functools.partial(state_kernel, float(channels * peers)),
        [(IN_VMEM, array) for array in (squares, value_early, value_late, steps)],
        [(IN_VMEM, (length * ROWS, LANES), F32), (IN_VMEM, flat, F32)],
        [pltpu.VMEM((length, LANES), F32)],
    )
    received = lax.all_to_all(
        states.reshape(shares), "ctx", split_axis=0, concat_axis=0, tiled=True
    )
    conv_inner, mode_weights, decay = call(
        "inner",
        functools.partial(inner_kernel, shares[1]),
        [
            (IN_SMEM, place),
            (IN_VMEM, u_two),
            (IN_VMEM, steps),
            (IN_HBM, li_rates),
            (IN_HBM, li_residues),
        ],
        [
            (IN_VMEM, (length * ROWS, LANES), F32),
            (IN_VMEM, flat, F32),
            (IN_VMEM, shares[1:], F32),
        ],
        [
            pltpu.VMEM((modes, channels), F32),
            pltpu.VMEM((modes, channels), F32),
            pltpu.VMEM(flat, F32),
            pltpu.SemaphoreType.DMA((2,)),
        ],
    )
    (entries,) = call(
        "scan",
        scan_kernel,
        [(IN_VMEM, received), (IN_VMEM, decay)],
        [(IN_VMEM, shares, F32)],
    )
    entries = lax.all_to_all(entries, "ctx", split_axis=0, concat_axis=0, tiled=True)
    (mixed,) = call(
        "output",
        output_kernel,
        [
            (IN_VMEM, array)
            for array in (entries.reshape(flat), conv_inner, steps, mode_weights, q_two)
        ],
        [(IN_HBM, (length, channels), BF16)],
        [
            pltpu.VMEM((length * ROWS, LANES), F32),
            pltpu.VMEM((length, channels), BF16),
            pltpu.SemaphoreType.DMA((QUARTERS,)),
        ],
    )
    return mixed


def solution(mesh):
    in_specs = (
        P("ctx", "tp"),
        P("ctx", "tp"),
        P("ctx", "tp"),
        P("tp", None),
        P("tp"),
        P("ctx", "tp"),
        P("ctx", "tp"),
        P(None, "tp"),
        P(None, "tp"),
    )
    return jax.shard_map(
        on_device, mesh=mesh, in_specs=in_specs, out_specs=P("ctx", "tp"), check_vma=False
    )
```

```python
import functools

import jax
import jax.numpy as jnp
from jax import lax
from jax.experimental import pallas as pl
from jax.experimental.pallas import tpu as pltpu
from jax.sharding import PartitionSpec as P

LANES = 128
ROWS = 8
BLOCK = 64
UNROLL = 8
CHUNK = 16
QUARTERS = 4
F32 = jnp.float32
BF16 = jnp.bfloat16
INTERPRET = False
IN_VMEM = pl.BlockSpec(memory_space=pltpu.VMEM)
IN_SMEM = pl.BlockSpec(memory_space=pltpu.SMEM)
IN_HBM = pl.BlockSpec(memory_space=pltpu.HBM)


def hbm(array):
    return array if INTERPRET else pltpu.with_memory_space_constraint(array, pltpu.HBM)


def call(name, kernel, inputs, outputs, scratch=()):
    return pl.pallas_call(
        kernel,
        out_shape=[jax.ShapeDtypeStruct(dims, kind) for _, dims, kind in outputs],
        in_specs=[spec for spec, _ in inputs],
        out_specs=[spec for spec, _, _ in outputs],
        scratch_shapes=list(scratch),
        compiler_params=pltpu.CompilerParams(vmem_limit_bytes=16 * 2**20),
        interpret=INTERPRET,
        name=name,
    )(*[hbm(array) if spec is IN_HBM else array for spec, array in inputs])


def fetch(pairs, sems):
    copies = [
        pltpu.make_async_copy(source, target, sems.at[i])
        for i, (source, target) in enumerate(pairs)
    ]
    for copy in copies:
        copy.start()
    return copies


def channel_rows(ref, table):
    modes = table.shape[0]
    for block in range(table.shape[1] // LANES):
        piece = table[:, block * LANES : (block + 1) * LANES]
        ref[pl.ds(block, modes, stride=ROWS), :] = piece


def one_minus_exp(x):
    total = jnp.full_like(x, 1.0)
    for order in range(11, 1, -1):
        total = 1.0 - total * x * (1.0 / order)
    return jnp.where(x < 0.5, x * total, 1.0 - jnp.exp(-x))


def product_bf16(left, right):
    return (left.astype(F32) * right.astype(F32)).astype(BF16)


def filtered(tap_ref, tile, per_tile, windows, member):
    conv = None
    for place in range(per_tile):
        taps = tap_ref[tile * per_tile + place, :, : windows.shape[0]]
        product = jnp.dot(taps, windows, preferred_element_type=F32)
        conv = product if place == 0 else jnp.where(member == place, product, conv)
    return conv


def gated(conv, tile, q, gate, gain, partial, value_ref):
    for part in range(2):
        rows = slice(part * BLOCK, (part + 1) * BLOCK)
        z_one = q[rows].astype(F32) * conv[:, part * LANES : (part + 1) * LANES]
        partial[part] = partial[part] + z_one * z_one
        value = gate[rows].astype(F32) * (z_one * gain)
        value_ref[pl.ds(part * BLOCK * ROWS + tile, BLOCK, stride=ROWS), :] = value


def token_row(partial):
    return jnp.sum(jnp.concatenate(partial, axis=0).T, axis=0, keepdims=True)


def lane_member(group_ch):
    lane = lax.broadcasted_iota(jnp.int32, (BLOCK, 2 * LANES), 1)
    return (lane & (LANES - 1)) // group_ch


def tail_kernel(k_hbm, v_hbm, tail_ref, k_ref, v_ref, sems):
    rows = pl.ds(k_hbm.shape[0] - tail_ref.shape[0], tail_ref.shape[0])
    for copy in fetch([(k_hbm.at[rows, :], k_ref), (v_hbm.at[rows, :], v_ref)], sems):
        copy.wait()
    tail_ref[...] = product_bf16(k_ref[...], v_ref[...])


def late_kernel(
    group_ch,
    share,
    place_ref,
    k_hbm,
    v_hbm,
    q_hbm,
    gate_hbm,
    filter_hbm,
    gain_hbm,
    rates_hbm,
    residues_hbm,
    tap_ref,
    conv_ref,
    q_early_ref,
    gate_early_ref,
    gain_ref,
    step_ref,
    weight_ref,
    decay_ref,
    value_ref,
    square_ref,
    k_ref,
    v_ref,
    q_ref,
    gate_ref,
    filter_ref,
    rates_ref,
    residues_ref,
    decays_ref,
    sems,
):
    length, channels = k_hbm.shape
    half = length // 2
    early, late = pl.ds(0, half), pl.ds(half, half)
    copies = fetch(
        [
            (filter_hbm, filter_ref),
            (k_hbm, k_ref),
            (v_hbm, v_ref),
            (q_hbm.at[late, :], q_ref),
            (gate_hbm.at[late, :], gate_ref),
            (gain_hbm, gain_ref),
            (rates_hbm, rates_ref),
            (residues_hbm, residues_ref),
            (q_hbm.at[early, :], q_early_ref),
            (gate_hbm.at[early, :], gate_early_ref),
        ],
        sems,
    )
    copies[0].wait()
    groups, taps = filter_ref.shape
    row = lax.broadcasted_iota(jnp.int32, (taps, taps), 0)
    col = lax.broadcasted_iota(jnp.int32, (taps, taps), 1)
    flip = jnp.where(((row + col) & (taps - 1)) == 0, 1.0, 0.0).astype(BF16)
    mirrored = jnp.dot(filter_ref[...], flip, preferred_element_type=F32)
    before = (col > row)[:BLOCK]
    for group in range(groups):
        line = jnp.broadcast_to(mirrored[group : group + 1, :], (BLOCK, taps))
        circulant = pltpu.roll(line, 0, axis=1, stride=1, stride_axis=0)
        tap_ref[group, :, :taps] = jnp.where(before, circulant, 0.0).astype(BF16)
        tap_ref[group, :, taps:] = jnp.where(before, 0.0, circulant).astype(BF16)
    for copy in copies[1:8]:
        copy.wait()
    rates = rates_ref[...]
    channel_rows(step_ref, jnp.exp(-rates))
    channel_rows(decays_ref, jnp.exp(-rates * float(length)))
    channel_rows(weight_ref, residues_ref[...] * jnp.sqrt(one_minus_exp(2.0 * rates)))
    decay_ref[...] = decays_ref[pl.ds(place_ref[0] * share, share), :]
    member = lane_member(group_ch)
    partial = [jnp.zeros((BLOCK, LANES), F32) for _ in range(2)]
    none = jnp.zeros((BLOCK, LANES), BF16)
    for tile in range(channels // LANES):
        cols = slice(tile * LANES, (tile + 1) * LANES)
        u_one = product_bf16(k_ref[:, cols], v_ref[:, cols])
        first = jnp.concatenate([none, none, u_one[:half]], axis=0)
        second = jnp.concatenate([none, u_one[: half + BLOCK]], axis=0)
        windows = jnp.concatenate([first, second], axis=1)
        conv_ref[tile] = filtered(tap_ref, tile, LANES // group_ch, windows, member)
        later = jnp.concatenate([u_one[BLOCK:], none], axis=0)
        windows = jnp.concatenate([u_one, later], axis=1)
        conv = filtered(tap_ref, tile, LANES // group_ch, windows, member)
        gated(conv, tile, q_ref[:, cols], gate_ref[:, cols], gain_ref[:, cols], partial, value_ref)
    square_ref[...] = token_row(partial)
    for copy in copies[8:]:
        copy.wait()


def early_kernel(
    group_ch,
    halo_ref,
    tap_ref,
    conv_ref,
    q_ref,
    gate_ref,
    gain_ref,
    late_ref,
    value_ref,
    square_ref,
):
    member = lane_member(group_ch)
    partial = [jnp.zeros((BLOCK, LANES), F32) for _ in range(2)]
    none = jnp.zeros((BLOCK, LANES), BF16)
    for tile in range(halo_ref.shape[1] // LANES):
        cols = slice(tile * LANES, (tile + 1) * LANES)
        halo = halo_ref[:, cols]
        second = jnp.concatenate([halo[BLOCK:], none], axis=0)
        windows = jnp.concatenate([halo, second], axis=1)
        conv = conv_ref[tile] + filtered(tap_ref, tile, LANES // group_ch, windows, member)
        gated(conv, tile, q_ref[:, cols], gate_ref[:, cols], gain_ref[:, cols], partial, value_ref)
    line = token_row(partial)
    for copy in range(square_ref.shape[0]):
        square_ref[copy, 0:1, :] = line
        square_ref[copy, 1:2, :] = late_ref[...]


def mode_rows(ref):
    return [ref[at : at + ROWS, :] for at in range(0, ref.shape[0], ROWS)]


def token_rows(t):
    return pl.ds(pl.multiple_of(t * ROWS, ROWS), ROWS)


def tree_sum(terms):
    while len(terms) > 1:
        terms = [x + y for x, y in zip(terms[::2], terms[1::2])]
    return terms[0]


def state_kernel(width, square_ref, early_ref, late_ref, step_ref, u_ref, state_ref, scale_ref):
    total = square_ref[0]
    for peer in range(1, square_ref.shape[0]):
        total = total + square_ref[peer]
    scale = lax.rsqrt(total / width + 1e-06)
    for part in range(2):
        line = jnp.broadcast_to(scale[part : part + 1, :], (LANES, LANES))
        scale_ref[part * LANES : (part + 1) * LANES, :] = line.T
    steps = mode_rows(step_ref)
    states = tuple(jnp.zeros((ROWS, LANES), F32) for _ in steps)
    for part, value_ref in enumerate((early_ref, late_ref)):

        def token(t, states):
            place = t + part * LANES
            factor = jnp.broadcast_to(scale_ref[pl.ds(place, 1), :], (ROWS, LANES))
            u_two = (value_ref[token_rows(t), :] * factor).astype(BF16).astype(F32)
            u_ref[token_rows(place), :] = u_two
            return tuple(a * s + u_two for a, s in zip(steps, states))

        states = lax.fori_loop(0, LANES, token, states, unroll=UNROLL)
    for m, state in enumerate(states):
        state_ref[m * ROWS : (m + 1) * ROWS, :] = state


def inner_kernel(u_ref, step_ref, weight_ref, decay_ref, conv_ref, decay_copy_ref):
    decay_copy_ref[...] = decay_ref[...]
    steps, weights = mode_rows(step_ref), mode_rows(weight_ref)

    def token(t, states):
        at = token_rows(t)
        u_two = u_ref[at, :]
        states = tuple(a * s + u_two for a, s in zip(steps, states))
        conv_ref[at, :] = tree_sum([w * s for w, s in zip(weights, states)])
        return states

    zero = tuple(jnp.zeros((ROWS, LANES), F32) for _ in steps)
    lax.fori_loop(0, u_ref.shape[0] // ROWS, token, zero, unroll=UNROLL)


def scan_kernel(state_ref, decay_ref, entry_ref):
    decay = decay_ref[...]
    entry = jnp.zeros_like(decay)
    for device in range(state_ref.shape[0]):
        entry_ref[device] = entry
        entry = decay * entry + state_ref[device]


def output_kernel(
    entry_ref, conv_ref, step_ref, weight_ref, gate_ref, out_hbm, sum_ref, out_ref, sems
):
    steps = mode_rows(step_ref)
    carried = tuple(w * e for w, e in zip(mode_rows(weight_ref), mode_rows(entry_ref)))
    length, channels = out_ref.shape

    def advance(chunk, carried):
        for t in range(CHUNK):
            carried = tuple(a * e for a, e in zip(steps, carried))
            at = token_rows(chunk * CHUNK + t)
            sum_ref[at, :] = conv_ref[at, :] + tree_sum(list(carried))
        return carried

    def emit(chunk):
        rows = pl.ds(pl.multiple_of(chunk * CHUNK, CHUNK), CHUNK)
        for tile in range(channels // LANES):
            cols = slice(tile * LANES, (tile + 1) * LANES)
            conv_two = sum_ref[pl.ds(chunk * (CHUNK * ROWS) + tile, CHUNK, stride=ROWS), :]
            out_ref[rows, cols] = (gate_ref[rows, cols].astype(F32) * conv_two).astype(BF16)

    def both(chunk, carried):
        emit(chunk - 1)
        return advance(chunk, carried)

    chunks = length // CHUNK
    per_quarter = chunks // QUARTERS
    copies = []
    carried = advance(0, carried)
    for quarter in range(QUARTERS):
        last = (quarter + 1) * per_quarter
        first = quarter * per_quarter + 1
        carried = lax.fori_loop(first, min(last + 1, chunks), both, carried)
        if last == chunks:
            emit(chunks - 1)
        rows = pl.ds(quarter * per_quarter * CHUNK, per_quarter * CHUNK)
        copy = pltpu.make_async_copy(out_ref.at[rows, :], out_hbm.at[rows, :], sems.at[quarter])
        copy.start()
        copies.append(copy)
    for copy in copies:
        copy.wait()


def on_device(q_one, k_one, v_one, mr_filter, norm_gain, q_two, k_two, li_rates, li_residues):
    length, channels = q_one.shape
    groups, taps = mr_filter.shape
    modes = li_rates.shape[0]
    devices, peers = lax.axis_size("ctx"), lax.axis_size("tp")
    group_ch = channels // groups
    half = length // 2
    flat = (modes * ROWS, LANES)
    shares = (devices, flat[0] // devices, LANES)
    place = lax.axis_index("ctx").astype(jnp.int32).reshape(1)

    (tail,) = call(
        "tail",
        tail_kernel,
        [(IN_HBM, k_one), (IN_HBM, v_one)],
        [(IN_VMEM, (taps, channels), BF16)],
        [pltpu.VMEM((taps, channels), BF16)] * 2 + [pltpu.SemaphoreType.DMA((2,))],
    )
    halo = lax.ppermute(tail, "ctx", [(i, i + 1) for i in range(devices - 1)])
    late = call(
        "late",
        functools.partial(late_kernel, group_ch, shares[1]),
        [
            (IN_SMEM, place),
            (IN_HBM, k_one),
            (IN_HBM, v_one),
            (IN_HBM, q_one),
            (IN_HBM, k_two),
            (IN_HBM, mr_filter),
            (IN_HBM, norm_gain[None, :]),
            (IN_HBM, li_rates),
            (IN_HBM, li_residues),
        ],
        [
            (IN_VMEM, (groups, BLOCK, 2 * taps), BF16),
            (IN_VMEM, (channels // LANES, BLOCK, 2 * LANES), F32),
            (IN_VMEM, (half, channels), BF16),
            (IN_VMEM, (half, channels), BF16),
            (IN_VMEM, (1, channels), F32),
            (IN_VMEM, flat, F32),
            (IN_VMEM, flat, F32),
            (IN_VMEM, shares[1:], F32),
            (IN_VMEM, (half * ROWS, LANES), F32),
            (IN_VMEM, (1, half), F32),
        ],
        [
            pltpu.VMEM((length, channels), BF16),
            pltpu.VMEM((length, channels), BF16),
            pltpu.VMEM((half, channels), BF16),
            pltpu.VMEM((half, channels), BF16),
            pltpu.VMEM((groups, taps), BF16),
            pltpu.VMEM((modes, channels), F32),
            pltpu.VMEM((modes, channels), F32),
            pltpu.VMEM(flat, F32),
            pltpu.SemaphoreType.DMA((10,)),
        ],
    )
    tap_table, conv_early, q_early, gate_early, gain, *late = late
    steps, mode_weights, decay, value_late, square_late = late
    value_early, squares = call(
        "early",
        functools.partial(early_kernel, group_ch),
        [
            (IN_VMEM, array)
            for array in (halo, tap_table, conv_early, q_early, gate_early, gain, square_late)
        ],
        [(IN_VMEM, (half * ROWS, LANES), F32), (IN_VMEM, (peers, 2, LANES), F32)],
    )
    squares = lax.all_to_all(squares, "tp", split_axis=0, concat_axis=0, tiled=True)
    u_two, states = call(
        "states",
        functools.partial(state_kernel, float(channels * peers)),
        [(IN_VMEM, array) for array in (squares, value_early, value_late, steps)],
        [(IN_VMEM, (length * ROWS, LANES), F32), (IN_VMEM, flat, F32)],
        [pltpu.VMEM((length, LANES), F32)],
    )
    received = lax.all_to_all(
        states.reshape(shares), "ctx", split_axis=0, concat_axis=0, tiled=True
    )
    conv_inner, decay = call(
        "inner",
        inner_kernel,
        [(IN_VMEM, array) for array in (u_two, steps, mode_weights, decay)],
        [(IN_VMEM, (length * ROWS, LANES), F32), (IN_VMEM, shares[1:], F32)],
    )
    (entries,) = call(
        "scan",
        scan_kernel,
        [(IN_VMEM, received), (IN_VMEM, decay)],
        [(IN_VMEM, shares, F32)],
    )
    entries = lax.all_to_all(entries, "ctx", split_axis=0, concat_axis=0, tiled=True)
    (mixed,) = call(
        "output",
        output_kernel,
        [
            (IN_VMEM, array)
            for array in (entries.reshape(flat), conv_inner, steps, mode_weights, q_two)
        ],
        [(IN_HBM, (length, channels), BF16)],
        [
            pltpu.VMEM((length * ROWS, LANES), F32),
            pltpu.VMEM((length, channels), BF16),
            pltpu.SemaphoreType.DMA((QUARTERS,)),
        ],
    )
    return mixed


def solution(mesh):
    in_specs = (
        P("ctx", "tp"),
        P("ctx", "tp"),
        P("ctx", "tp"),
        P("tp", None),
        P("tp"),
        P("ctx", "tp"),
        P("ctx", "tp"),
        P(None, "tp"),
        P(None, "tp"),
    )
    return jax.shard_map(
        on_device, mesh=mesh, in_specs=in_specs, out_specs=P("ctx", "tp"), check_vma=False
    )
```

```python
import functools

import jax
import jax.numpy as jnp
from jax import lax
from jax.experimental import pallas as pl
from jax.experimental.pallas import tpu as pltpu
from jax.sharding import PartitionSpec as P


LANES = 128
ROWS = 8
BLOCK = 64
UNROLL = 8
CHUNK = 16
QUARTERS = 4
F32 = jnp.float32
BF16 = jnp.bfloat16
INTERPRET = False
IN_VMEM = pl.BlockSpec(memory_space=pltpu.VMEM)
IN_SMEM = pl.BlockSpec(memory_space=pltpu.SMEM)
IN_HBM = pl.BlockSpec(memory_space=pltpu.HBM)


def hbm(array):
    return array if INTERPRET else pltpu.with_memory_space_constraint(array, pltpu.HBM)


def call(kernel, inputs, outputs, scratch=()):
    return pl.pallas_call(
        kernel,
        out_shape=[jax.ShapeDtypeStruct(dims, kind) for _, dims, kind in outputs],
        in_specs=[spec for spec, _ in inputs],
        out_specs=[spec for spec, _, _ in outputs],
        scratch_shapes=list(scratch),
        compiler_params=pltpu.CompilerParams(vmem_limit_bytes=16 * 2**20),
        interpret=INTERPRET,
    )(*[hbm(array) if spec is IN_HBM else array for spec, array in inputs])


def fetch(pairs, sems, start=0):
    copies = [
        pltpu.make_async_copy(source, target, sems.at[start + i])
        for i, (source, target) in enumerate(pairs)
    ]
    for copy in copies:
        copy.start()
    return copies


def channel_rows(ref, table):
    modes = table.shape[0]
    for block in range(table.shape[1] // LANES):
        piece = table[:, block * LANES : (block + 1) * LANES]
        ref[pl.ds(block, modes, stride=ROWS), :] = piece


def one_minus_exp(x):
    total = jnp.full_like(x, 1.0)
    for order in range(11, 1, -1):
        total = 1.0 - total * x * (1.0 / order)
    return jnp.where(x < 0.5, x * total, 1.0 - jnp.exp(-x))


def product_bf16(left, right):
    return (left.astype(F32) * right.astype(F32)).astype(BF16)


def filtered(tap_ref, tile, per_tile, windows, member):
    conv = None
    for place in range(per_tile):
        taps = tap_ref[tile * per_tile + place, :, : windows.shape[0]]
        product = jnp.dot(taps, windows, preferred_element_type=F32)
        conv = product if place == 0 else jnp.where(member == place, product, conv)
    return conv


def gated(conv, tile, q, gate, gain, partial, value_ref):
    for part in range(2):
        rows = slice(part * BLOCK, (part + 1) * BLOCK)
        z_one = q[rows].astype(F32) * conv[:, part * LANES : (part + 1) * LANES]
        partial[part] = partial[part] + z_one * z_one
        value = gate[rows].astype(F32) * (z_one * gain)
        value_ref[pl.ds(part * BLOCK * ROWS + tile, BLOCK, stride=ROWS), :] = value


def token_row(partial):
    return jnp.sum(jnp.concatenate(partial, axis=0).T, axis=0, keepdims=True)


def lane_member(group_ch):
    lane = lax.broadcasted_iota(jnp.int32, (BLOCK, 2 * LANES), 1)
    return (lane & (LANES - 1)) // group_ch


def tail_kernel(sender, place_ref, k_hbm, v_hbm, tail_ref, k_ref, v_ref, sems):
    @pl.when((place_ref[0] & 1) == sender)
    def _():
        rows = pl.ds(k_hbm.shape[0] - tail_ref.shape[0], tail_ref.shape[0])
        for copy in fetch([(k_hbm.at[rows, :], k_ref), (v_hbm.at[rows, :], v_ref)], sems):
            copy.wait()
        tail_ref[...] = product_bf16(k_ref[...], v_ref[...])


def late_kernel(
    group_ch,
    share,
    place_ref,
    k_hbm,
    v_hbm,
    q_hbm,
    gate_hbm,
    filter_hbm,
    gain_hbm,
    rates_hbm,
    residues_hbm,
    tap_ref,
    conv_ref,
    q_early_ref,
    gate_early_ref,
    gain_ref,
    step_ref,
    weight_ref,
    decay_ref,
    value_ref,
    square_ref,
    k_ref,
    v_ref,
    u_ref,
    q_ref,
    gate_ref,
    filter_ref,
    rates_ref,
    residues_ref,
    decays_ref,
    sems,
):
    length, channels = k_hbm.shape
    half = length // 2
    early, late = pl.ds(0, half), pl.ds(half, half)
    copies = fetch(
        [
            (filter_hbm, filter_ref),
            (k_hbm, k_ref),
            (v_hbm, v_ref),
            (rates_hbm, rates_ref),
            (residues_hbm, residues_ref),
        ],
        sems,
        0,
    )
    copies[0].wait()
    groups, taps = filter_ref.shape
    row = lax.broadcasted_iota(jnp.int32, (taps, taps), 0)
    col = lax.broadcasted_iota(jnp.int32, (taps, taps), 1)
    flip = jnp.where(((row + col) & (taps - 1)) == 0, 1.0, 0.0).astype(BF16)
    mirrored = jnp.dot(filter_ref[...], flip, preferred_element_type=F32)
    before = (col > row)[:BLOCK]
    zero = jnp.zeros((BLOCK, taps), BF16)
    for group in range(groups):
        line = jnp.broadcast_to(mirrored[group : group + 1, :], (BLOCK, taps))
        circulant = pltpu.roll(line, 0, axis=1, stride=1, stride_axis=0).astype(BF16)
        tap_ref[group, :, :taps] = jnp.where(before, circulant, zero)
        tap_ref[group, :, taps:] = jnp.where(before, zero, circulant)
    gates = fetch(
        [
            (q_hbm.at[late, :], q_ref),
            (gate_hbm.at[late, :], gate_ref),
            (gain_hbm, gain_ref),
            (q_hbm.at[early, :], q_early_ref),
            (gate_hbm.at[early, :], gate_early_ref),
        ],
        sems,
        len(copies),
    )
    for copy in copies[3:]:
        copy.wait()
    rates = rates_ref[...]
    channel_rows(step_ref, jnp.exp(-rates))
    channel_rows(decays_ref, jnp.exp(-rates * float(length)))
    channel_rows(weight_ref, residues_ref[...] * jnp.sqrt(one_minus_exp(2.0 * rates)))
    decay_ref[...] = decays_ref[pl.ds(place_ref[0] * share, share), :]
    for copy in copies[1:3]:
        copy.wait()
    member = lane_member(group_ch)
    per_tile = LANES // group_ch
    none = jnp.zeros((BLOCK, LANES), BF16)
    tiles = [slice(at, at + LANES) for at in range(0, channels, LANES)]
    for tile, cols in enumerate(tiles):
        u_one = product_bf16(k_ref[:, cols], v_ref[:, cols])
        u_ref[:, cols] = u_one
        first = jnp.concatenate([none, none, u_one[:BLOCK]], axis=0)
        second = jnp.concatenate([none, u_one[:half]], axis=0)
        windows = jnp.concatenate([first, second], axis=1)
        conv_ref[tile] = filtered(tap_ref, tile, per_tile, windows, member)
    for copy in gates:
        copy.wait()
    partial = [jnp.zeros((BLOCK, LANES), F32) for _ in range(2)]
    for tile, cols in enumerate(tiles):
        u_one = u_ref[:, cols]
        windows = jnp.concatenate([u_one[: taps + BLOCK], u_one[BLOCK:]], axis=1)
        conv = filtered(tap_ref, tile, per_tile, windows, member)
        gated(conv, tile, q_ref[:, cols], gate_ref[:, cols], gain_ref[:, cols], partial, value_ref)
    square_ref[...] = token_row(partial)


def early_kernel(
    group_ch,
    place_ref,
    far_ref,
    near_ref,
    tap_ref,
    conv_ref,
    q_ref,
    gate_ref,
    gain_ref,
    late_ref,
    value_ref,
    square_ref,
):
    member = lane_member(group_ch)
    partial = [jnp.zeros((BLOCK, LANES), F32) for _ in range(2)]
    none = jnp.zeros((BLOCK, LANES), BF16)
    far = (place_ref[0] & 1) == 0
    for tile in range(far_ref.shape[1] // LANES):
        cols = slice(tile * LANES, (tile + 1) * LANES)
        halo = jnp.where(far, far_ref[:, cols], near_ref[:, cols])
        second = jnp.concatenate([halo[BLOCK:], none], axis=0)
        windows = jnp.concatenate([halo, second], axis=1)
        conv = conv_ref[tile] + filtered(tap_ref, tile, LANES // group_ch, windows, member)
        gated(conv, tile, q_ref[:, cols], gate_ref[:, cols], gain_ref[:, cols], partial, value_ref)
    line = token_row(partial)
    for copy in range(square_ref.shape[0]):
        square_ref[copy, 0:1, :] = line
        square_ref[copy, 1:2, :] = late_ref[...]


def mode_rows(ref):
    return [ref[at : at + ROWS, :] for at in range(0, ref.shape[0], ROWS)]


def token_rows(t):
    return pl.ds(pl.multiple_of(t * ROWS, ROWS), ROWS)


def tree_sum(terms):
    while len(terms) > 1:
        terms = [x + y for x, y in zip(terms[::2], terms[1::2])]
    return terms[0]


def state_kernel(width, square_ref, early_ref, late_ref, step_ref, u_ref, state_ref, scale_ref):
    total = square_ref[0]
    for peer in range(1, square_ref.shape[0]):
        total = total + square_ref[peer]
    scale = lax.rsqrt(total / width + 1e-06)
    for part in range(2):
        line = jnp.broadcast_to(scale[part : part + 1, :], (LANES, LANES))
        scale_ref[part * LANES : (part + 1) * LANES, :] = line.T
    steps = mode_rows(step_ref)
    states = tuple(jnp.zeros((ROWS, LANES), F32) for _ in steps)
    for part, value_ref in enumerate((early_ref, late_ref)):

        def token(t, states):
            place = t + part * LANES
            factor = jnp.broadcast_to(scale_ref[pl.ds(place, 1), :], (ROWS, LANES))
            u_two = (value_ref[token_rows(t), :] * factor).astype(BF16).astype(F32)
            u_ref[token_rows(place), :] = u_two
            return tuple(a * s + u_two for a, s in zip(steps, states))

        states = lax.fori_loop(0, LANES, token, states, unroll=UNROLL)
    for m, state in enumerate(states):
        state_ref[m * ROWS : (m + 1) * ROWS, :] = state


def inner_kernel(u_ref, step_ref, weight_ref, decay_ref, conv_ref, decay_copy_ref):
    decay_copy_ref[...] = decay_ref[...]
    steps, weights = mode_rows(step_ref), mode_rows(weight_ref)

    def token(t, states):
        at = token_rows(t)
        u_two = u_ref[at, :]
        states = tuple(a * s + u_two for a, s in zip(steps, states))
        conv_ref[at, :] = tree_sum([w * s for w, s in zip(weights, states)])
        return states

    zero = tuple(jnp.zeros((ROWS, LANES), F32) for _ in steps)
    lax.fori_loop(0, u_ref.shape[0] // ROWS, token, zero, unroll=UNROLL)


def scan_kernel(state_ref, decay_ref, entry_ref):
    decay = decay_ref[...]
    entry = jnp.zeros_like(decay)
    for device in range(state_ref.shape[0]):
        entry_ref[device] = entry
        entry = decay * entry + state_ref[device]


def output_kernel(
    entry_ref, conv_ref, step_ref, weight_ref, gate_ref, out_hbm, sum_ref, out_ref, sems
):
    steps = mode_rows(step_ref)
    carried = tuple(w * e for w, e in zip(mode_rows(weight_ref), mode_rows(entry_ref)))
    length, channels = out_ref.shape

    def advance(chunk, carried):
        for t in range(CHUNK):
            carried = tuple(a * e for a, e in zip(steps, carried))
            at = token_rows(chunk * CHUNK + t)
            sum_ref[at, :] = conv_ref[at, :] + tree_sum(list(carried))
        return carried

    def emit(chunk):
        rows = pl.ds(pl.multiple_of(chunk * CHUNK, CHUNK), CHUNK)
        for tile in range(channels // LANES):
            cols = slice(tile * LANES, (tile + 1) * LANES)
            conv_two = sum_ref[pl.ds(chunk * (CHUNK * ROWS) + tile, CHUNK, stride=ROWS), :]
            out_ref[rows, cols] = (gate_ref[rows, cols].astype(F32) * conv_two).astype(BF16)

    def both(chunk, carried):
        emit(chunk - 1)
        return advance(chunk, carried)

    chunks = length // CHUNK
    per_quarter = chunks // QUARTERS
    copies = []
    carried = advance(0, carried)
    for quarter in range(QUARTERS):
        last = (quarter + 1) * per_quarter
        first = quarter * per_quarter + 1
        carried = lax.fori_loop(first, min(last + 1, chunks), both, carried)
        if last == chunks:
            emit(chunks - 1)
        rows = pl.ds(quarter * per_quarter * CHUNK, per_quarter * CHUNK)
        copy = pltpu.make_async_copy(out_ref.at[rows, :], out_hbm.at[rows, :], sems.at[quarter])
        copy.start()
        copies.append(copy)
    for copy in copies:
        copy.wait()


def on_device(q_one, k_one, v_one, mr_filter, norm_gain, q_two, k_two, li_rates, li_residues):
    length, channels = q_one.shape
    groups, taps = mr_filter.shape
    modes = li_rates.shape[0]
    devices, peers = lax.axis_size("ctx"), lax.axis_size("tp")
    group_ch = channels // groups
    half = length // 2
    flat = (modes * ROWS, LANES)
    shares = (devices, flat[0] // devices, LANES)
    place = lax.axis_index("ctx").astype(jnp.int32).reshape(1)

    def passed_on(sender):
        (tail,) = call(
            functools.partial(tail_kernel, sender),
            [(IN_SMEM, place), (IN_HBM, k_one), (IN_HBM, v_one)],
            [(IN_VMEM, (taps, channels), BF16)],
            [pltpu.VMEM((taps, channels), BF16)] * 2 + [pltpu.SemaphoreType.DMA((2,))],
        )
        return lax.ppermute(tail, "ctx", [(i, i + 1) for i in range(sender, devices - 1, 2)])

    far_halo, near_halo = passed_on(1), passed_on(0)
    late = call(
        functools.partial(late_kernel, group_ch, shares[1]),
        [
            (IN_SMEM, place),
            (IN_HBM, k_one),
            (IN_HBM, v_one),
            (IN_HBM, q_one),
            (IN_HBM, k_two),
            (IN_HBM, mr_filter),
            (IN_HBM, norm_gain[None, :]),
            (IN_HBM, li_rates),
            (IN_HBM, li_residues),
        ],
        [
            (IN_VMEM, (groups, BLOCK, 2 * taps), BF16),
            (IN_VMEM, (channels // LANES, BLOCK, 2 * LANES), F32),
            (IN_VMEM, (half, channels), BF16),
            (IN_VMEM, (half, channels), BF16),
            (IN_VMEM, (1, channels), F32),
            (IN_VMEM, flat, F32),
            (IN_VMEM, flat, F32),
            (IN_VMEM, shares[1:], F32),
            (IN_VMEM, (half * ROWS, LANES), F32),
            (IN_VMEM, (1, half), F32),
        ],
        [
            pltpu.VMEM((length, channels), BF16),
            pltpu.VMEM((length, channels), BF16),
            pltpu.VMEM((length, channels), BF16),
            pltpu.VMEM((half, channels), BF16),
            pltpu.VMEM((half, channels), BF16),
            pltpu.VMEM((groups, taps), BF16),
            pltpu.VMEM((modes, channels), F32),
            pltpu.VMEM((modes, channels), F32),
            pltpu.VMEM(flat, F32),
            pltpu.SemaphoreType.DMA((10,)),
        ],
    )
    tap_table, conv_early, q_early, gate_early, gain, *late = late
    steps, mode_weights, decay, value_late, square_late = late
    value_early, squares = call(
        functools.partial(early_kernel, group_ch),
        [(IN_SMEM, place)]
        + [
            (IN_VMEM, array)
            for array in (far_halo, near_halo, tap_table, conv_early, q_early, gate_early, gain, square_late)
        ],
        [(IN_VMEM, (half * ROWS, LANES), F32), (IN_VMEM, (peers, 2, LANES), F32)],
    )
    squares = lax.all_to_all(squares, "tp", split_axis=0, concat_axis=0, tiled=True)
    u_two, states = call(
        functools.partial(state_kernel, float(channels * peers)),
        [(IN_VMEM, array) for array in (squares, value_early, value_late, steps)],
        [(IN_VMEM, (length * ROWS, LANES), F32), (IN_VMEM, flat, F32)],
        [pltpu.VMEM((length, LANES), F32)],
    )
    received = lax.all_to_all(
        states.reshape(shares), "ctx", split_axis=0, concat_axis=0, tiled=True
    )
    conv_inner, decay = call(
        inner_kernel,
        [(IN_VMEM, array) for array in (u_two, steps, mode_weights, decay)],
        [(IN_VMEM, (length * ROWS, LANES), F32), (IN_VMEM, shares[1:], F32)],
    )
    (entries,) = call(
        scan_kernel, [(IN_VMEM, received), (IN_VMEM, decay)], [(IN_VMEM, shares, F32)]
    )
    entries = lax.all_to_all(entries, "ctx", split_axis=0, concat_axis=0, tiled=True)
    (mixed,) = call(
        output_kernel,
        [
            (IN_VMEM, array)
            for array in (entries.reshape(flat), conv_inner, steps, mode_weights, q_two)
        ],
        [(IN_HBM, (length, channels), BF16)],
        [
            pltpu.VMEM((length * ROWS, LANES), F32),
            pltpu.VMEM((length, channels), BF16),
            pltpu.SemaphoreType.DMA((QUARTERS,)),
        ],
    )
    return mixed


def solution(mesh):
    in_specs = (
        P("ctx", "tp"),
        P("ctx", "tp"),
        P("ctx", "tp"),
        P("tp", None),
        P("tp"),
        P("ctx", "tp"),
        P("ctx", "tp"),
        P(None, "tp"),
        P(None, "tp"),
    )
    return jax.shard_map(
        on_device, mesh=mesh, in_specs=in_specs, out_specs=P("ctx", "tp"), check_vma=False
    )
```

```python
import functools

import jax
import jax.numpy as jnp
from jax import lax
from jax.experimental import pallas as pl
from jax.experimental.pallas import tpu as pltpu
from jax.sharding import PartitionSpec as P


LANES = 128
ROWS = 8
BLOCK = 64
UNROLL = 16
CHUNK = 16
QUARTERS = 8
F32 = jnp.float32
BF16 = jnp.bfloat16
INTERPRET = False
IN_VMEM = pl.BlockSpec(memory_space=pltpu.VMEM)
IN_SMEM = pl.BlockSpec(memory_space=pltpu.SMEM)
IN_HBM = pl.BlockSpec(memory_space=pltpu.HBM)


def hbm(array):
    return array if INTERPRET else pltpu.with_memory_space_constraint(array, pltpu.HBM)


def call(kernel, inputs, outputs, scratch=()):
    return pl.pallas_call(
        kernel,
        out_shape=[jax.ShapeDtypeStruct(dims, kind) for _, dims, kind in outputs],
        in_specs=[spec for spec, _ in inputs],
        out_specs=[spec for spec, _, _ in outputs],
        scratch_shapes=list(scratch),
        compiler_params=pltpu.CompilerParams(vmem_limit_bytes=16 * 2**20),
        interpret=INTERPRET,
    )(*[hbm(array) if spec is IN_HBM else array for spec, array in inputs])


def fetch(pairs, sems):
    copies = [
        pltpu.make_async_copy(source, target, sems.at[i])
        for i, (source, target) in enumerate(pairs)
    ]
    for copy in copies:
        copy.start()
    return copies


def channel_rows(ref, table):
    modes = table.shape[0]
    for block in range(table.shape[1] // LANES):
        piece = table[:, block * LANES : (block + 1) * LANES]
        ref[pl.ds(block, modes, stride=ROWS), :] = piece


def one_minus_exp(x):
    total = jnp.full_like(x, 1.0)
    for order in range(11, 1, -1):
        total = 1.0 - total * x * (1.0 / order)
    return jnp.where(x < 0.5, x * total, 1.0 - jnp.exp(-x))


def product_bf16(left, right):
    return (left.astype(F32) * right.astype(F32)).astype(BF16)


def filtered(tap_ref, tile, per_tile, windows, member):
    conv = None
    for place in range(per_tile):
        taps = tap_ref[tile * per_tile + place, :, : windows.shape[0]]
        product = jnp.dot(taps, windows, preferred_element_type=F32)
        conv = product if place == 0 else jnp.where(member == place, product, conv)
    return conv


def gated(conv, tile, q, gate, gain, partial, value_ref):
    for part in range(2):
        rows = slice(part * BLOCK, (part + 1) * BLOCK)
        z_one = q[rows].astype(F32) * conv[:, part * LANES : (part + 1) * LANES]
        partial[part] = partial[part] + z_one * z_one
        value = gate[rows].astype(F32) * (z_one * gain)
        value_ref[pl.ds(part * BLOCK * ROWS + tile, BLOCK, stride=ROWS), :] = value


def token_row(partial):
    return jnp.sum(jnp.concatenate(partial, axis=0).T, axis=0, keepdims=True)


def lane_member(group_ch):
    lane = lax.broadcasted_iota(jnp.int32, (BLOCK, 2 * LANES), 1)
    return (lane & (LANES - 1)) // group_ch


def tail_kernel(sender, place_ref, k_hbm, v_hbm, tail_ref, k_ref, v_ref, sems):
    @pl.when((place_ref[0] & 1) == sender)
    def _():
        rows = pl.ds(k_hbm.shape[0] - tail_ref.shape[0], tail_ref.shape[0])
        for copy in fetch([(k_hbm.at[rows, :], k_ref), (v_hbm.at[rows, :], v_ref)], sems):
            copy.wait()
        tail_ref[...] = product_bf16(k_ref[...], v_ref[...])


def late_kernel(
    group_ch,
    share,
    place_ref,
    k_hbm,
    v_hbm,
    q_hbm,
    gate_hbm,
    filter_hbm,
    gain_hbm,
    rates_hbm,
    residues_hbm,
    tap_ref,
    conv_ref,
    q_early_ref,
    gate_early_ref,
    gain_ref,
    step_ref,
    weight_ref,
    decay_ref,
    value_ref,
    square_ref,
    k_ref,
    v_ref,
    q_ref,
    gate_ref,
    filter_ref,
    rates_ref,
    residues_ref,
    decays_ref,
    sems,
):
    length, channels = k_hbm.shape
    half = length // 2
    early, late = pl.ds(0, half), pl.ds(half, half)
    copies = fetch(
        [
            (filter_hbm, filter_ref),
            (rates_hbm, rates_ref),
            (residues_hbm, residues_ref),
            (k_hbm, k_ref),
            (v_hbm, v_ref),
            (q_hbm.at[late, :], q_ref),
            (gate_hbm.at[late, :], gate_ref),
            (gain_hbm, gain_ref),
            (q_hbm.at[early, :], q_early_ref),
            (gate_hbm.at[early, :], gate_early_ref),
        ],
        sems,
    )
    copies[0].wait()
    groups, taps = filter_ref.shape
    row = lax.broadcasted_iota(jnp.int32, (taps, taps), 0)
    col = lax.broadcasted_iota(jnp.int32, (taps, taps), 1)
    flip = jnp.where(((row + col) & (taps - 1)) == 0, 1.0, 0.0).astype(BF16)
    mirrored = jnp.dot(filter_ref[...], flip, preferred_element_type=F32)
    before = (col > row)[:BLOCK]
    zero = jnp.zeros((BLOCK, taps), BF16)
    for group in range(groups):
        line = jnp.broadcast_to(mirrored[group : group + 1, :], (BLOCK, taps))
        circulant = pltpu.roll(line, 0, axis=1, stride=1, stride_axis=0).astype(BF16)
        tap_ref[group, :, :taps] = jnp.where(before, circulant, zero)
        tap_ref[group, :, taps:] = jnp.where(before, zero, circulant)
    for copy in copies[1:3]:
        copy.wait()
    rates = rates_ref[...]
    channel_rows(step_ref, jnp.exp(-rates))
    channel_rows(decays_ref, jnp.exp(-rates * float(length)))
    channel_rows(weight_ref, residues_ref[...] * jnp.sqrt(one_minus_exp(2.0 * rates)))
    decay_ref[...] = decays_ref[pl.ds(place_ref[0] * share, share), :]
    for copy in copies[3:8]:
        copy.wait()
    member = lane_member(group_ch)
    partial = [jnp.zeros((BLOCK, LANES), F32) for _ in range(2)]
    none = jnp.zeros((BLOCK, LANES), BF16)
    for tile in range(channels // LANES):
        cols = slice(tile * LANES, (tile + 1) * LANES)
        u_one = product_bf16(k_ref[:, cols], v_ref[:, cols])
        first = jnp.concatenate([none, none, u_one[:BLOCK]], axis=0)
        second = jnp.concatenate([none, u_one[:half]], axis=0)
        windows = jnp.concatenate([first, second], axis=1)
        conv_ref[tile] = filtered(tap_ref, tile, LANES // group_ch, windows, member)
        windows = jnp.concatenate([u_one[: taps + BLOCK], u_one[BLOCK:]], axis=1)
        conv = filtered(tap_ref, tile, LANES // group_ch, windows, member)
        gated(conv, tile, q_ref[:, cols], gate_ref[:, cols], gain_ref[:, cols], partial, value_ref)
    square_ref[...] = token_row(partial)
    for copy in copies[8:]:
        copy.wait()


def early_kernel(
    group_ch,
    place_ref,
    far_ref,
    near_ref,
    tap_ref,
    conv_ref,
    q_ref,
    gate_ref,
    gain_ref,
    late_ref,
    value_ref,
    square_ref,
):
    member = lane_member(group_ch)
    partial = [jnp.zeros((BLOCK, LANES), F32) for _ in range(2)]
    none = jnp.zeros((BLOCK, LANES), BF16)
    far = (place_ref[0] & 1) == 0
    for tile in range(far_ref.shape[1] // LANES):
        cols = slice(tile * LANES, (tile + 1) * LANES)
        halo = jnp.where(far, far_ref[:, cols], near_ref[:, cols])
        second = jnp.concatenate([halo[BLOCK:], none], axis=0)
        windows = jnp.concatenate([halo, second], axis=1)
        conv = conv_ref[tile] + filtered(tap_ref, tile, LANES // group_ch, windows, member)
        gated(conv, tile, q_ref[:, cols], gate_ref[:, cols], gain_ref[:, cols], partial, value_ref)
    line = token_row(partial)
    for copy in range(square_ref.shape[0]):
        square_ref[copy, 0:1, :] = line
        square_ref[copy, 1:2, :] = late_ref[...]


def mode_rows(ref):
    return [ref[at : at + ROWS, :] for at in range(0, ref.shape[0], ROWS)]


def token_rows(t):
    return pl.ds(pl.multiple_of(t * ROWS, ROWS), ROWS)


def tree_sum(terms):
    while len(terms) > 1:
        terms = [x + y for x, y in zip(terms[::2], terms[1::2])]
    return terms[0]


def state_kernel(width, square_ref, early_ref, late_ref, step_ref, u_ref, state_ref, scale_ref):
    total = square_ref[0]
    for peer in range(1, square_ref.shape[0]):
        total = total + square_ref[peer]
    scale = lax.rsqrt(total / width + 1e-06)
    for part in range(2):
        line = jnp.broadcast_to(scale[part : part + 1, :], (LANES, LANES))
        scale_ref[part * LANES : (part + 1) * LANES, :] = line.T
    steps = mode_rows(step_ref)
    states = tuple(jnp.zeros((ROWS, LANES), F32) for _ in steps)
    for part, value_ref in enumerate((early_ref, late_ref)):

        def token(t, states):
            place = t + part * LANES
            factor = jnp.broadcast_to(scale_ref[pl.ds(place, 1), :], (ROWS, LANES))
            u_two = (value_ref[token_rows(t), :] * factor).astype(BF16).astype(F32)
            u_ref[token_rows(place), :] = u_two
            return tuple(a * s + u_two for a, s in zip(steps, states))

        states = lax.fori_loop(0, LANES, token, states, unroll=UNROLL)
    for m, state in enumerate(states):
        state_ref[m * ROWS : (m + 1) * ROWS, :] = state


def inner_kernel(u_ref, step_ref, weight_ref, decay_ref, conv_ref, decay_copy_ref):
    decay_copy_ref[...] = decay_ref[...]
    steps, weights = mode_rows(step_ref), mode_rows(weight_ref)

    def token(t, states):
        at = token_rows(t)
        u_two = u_ref[at, :]
        states = tuple(a * s + u_two for a, s in zip(steps, states))
        conv_ref[at, :] = tree_sum([w * s for w, s in zip(weights, states)])
        return states

    zero = tuple(jnp.zeros((ROWS, LANES), F32) for _ in steps)
    lax.fori_loop(0, u_ref.shape[0] // ROWS, token, zero, unroll=UNROLL)


def scan_kernel(state_ref, decay_ref, entry_ref):
    decay = decay_ref[...]
    entry = jnp.zeros_like(decay)
    for device in range(state_ref.shape[0]):
        entry_ref[device] = entry
        entry = decay * entry + state_ref[device]


def output_kernel(
    entry_ref, conv_ref, step_ref, weight_ref, gate_ref, out_hbm, sum_ref, out_ref, sems
):
    steps = mode_rows(step_ref)
    carried = tuple(w * e for w, e in zip(mode_rows(weight_ref), mode_rows(entry_ref)))
    length, channels = out_ref.shape

    def advance(chunk, carried):
        for t in range(CHUNK):
            carried = tuple(a * e for a, e in zip(steps, carried))
            at = token_rows(chunk * CHUNK + t)
            sum_ref[at, :] = conv_ref[at, :] + tree_sum(list(carried))
        return carried

    def emit(chunk):
        rows = pl.ds(pl.multiple_of(chunk * CHUNK, CHUNK), CHUNK)
        for tile in range(channels // LANES):
            cols = slice(tile * LANES, (tile + 1) * LANES)
            conv_two = sum_ref[pl.ds(chunk * (CHUNK * ROWS) + tile, CHUNK, stride=ROWS), :]
            out_ref[rows, cols] = (gate_ref[rows, cols].astype(F32) * conv_two).astype(BF16)

    def both(chunk, carried):
        emit(chunk - 1)
        return advance(chunk, carried)

    chunks = length // CHUNK
    per_quarter = chunks // QUARTERS
    copies = []
    carried = advance(0, carried)
    for quarter in range(QUARTERS):
        last = (quarter + 1) * per_quarter
        first = quarter * per_quarter + 1
        carried = lax.fori_loop(first, min(last + 1, chunks), both, carried)
        if last == chunks:
            emit(chunks - 1)
        rows = pl.ds(quarter * per_quarter * CHUNK, per_quarter * CHUNK)
        copy = pltpu.make_async_copy(out_ref.at[rows, :], out_hbm.at[rows, :], sems.at[quarter])
        copy.start()
        copies.append(copy)
    for copy in copies:
        copy.wait()


def on_device(q_one, k_one, v_one, mr_filter, norm_gain, q_two, k_two, li_rates, li_residues):
    length, channels = q_one.shape
    groups, taps = mr_filter.shape
    modes = li_rates.shape[0]
    devices, peers = lax.axis_size("ctx"), lax.axis_size("tp")
    group_ch = channels // groups
    half = length // 2
    flat = (modes * ROWS, LANES)
    shares = (devices, flat[0] // devices, LANES)
    place = lax.axis_index("ctx").astype(jnp.int32).reshape(1)

    def passed_on(sender):
        (tail,) = call(
            functools.partial(tail_kernel, sender),
            [(IN_SMEM, place), (IN_HBM, k_one), (IN_HBM, v_one)],
            [(IN_VMEM, (taps, channels), BF16)],
            [pltpu.VMEM((taps, channels), BF16)] * 2 + [pltpu.SemaphoreType.DMA((2,))],
        )
        return lax.ppermute(tail, "ctx", [(i, i + 1) for i in range(sender, devices - 1, 2)])

    far_halo, near_halo = passed_on(1), passed_on(0)
    late = call(
        functools.partial(late_kernel, group_ch, shares[1]),
        [
            (IN_SMEM, place),
            (IN_HBM, k_one),
            (IN_HBM, v_one),
            (IN_HBM, q_one),
            (IN_HBM, k_two),
            (IN_HBM, mr_filter),
            (IN_HBM, norm_gain[None, :]),
            (IN_HBM, li_rates),
            (IN_HBM, li_residues),
        ],
        [
            (IN_VMEM, (groups, BLOCK, 2 * taps), BF16),
            (IN_VMEM, (channels // LANES, BLOCK, 2 * LANES), F32),
            (IN_VMEM, (half, channels), BF16),
            (IN_VMEM, (half, channels), BF16),
            (IN_VMEM, (1, channels), F32),
            (IN_VMEM, flat, F32),
            (IN_VMEM, flat, F32),
            (IN_VMEM, shares[1:], F32),
            (IN_VMEM, (half * ROWS, LANES), F32),
            (IN_VMEM, (1, half), F32),
        ],
        [
            pltpu.VMEM((length, channels), BF16),
            pltpu.VMEM((length, channels), BF16),
            pltpu.VMEM((half, channels), BF16),
            pltpu.VMEM((half, channels), BF16),
            pltpu.VMEM((groups, taps), BF16),
            pltpu.VMEM((modes, channels), F32),
            pltpu.VMEM((modes, channels), F32),
            pltpu.VMEM(flat, F32),
            pltpu.SemaphoreType.DMA((10,)),
        ],
    )
    tap_table, conv_early, q_early, gate_early, gain, *late = late
    steps, mode_weights, decay, value_late, square_late = late
    value_early, squares = call(
        functools.partial(early_kernel, group_ch),
        [(IN_SMEM, place)]
        + [
            (IN_VMEM, array)
            for array in (far_halo, near_halo, tap_table, conv_early, q_early, gate_early, gain, square_late)
        ],
        [(IN_VMEM, (half * ROWS, LANES), F32), (IN_VMEM, (peers, 2, LANES), F32)],
    )
    squares = lax.all_to_all(squares, "tp", split_axis=0, concat_axis=0, tiled=True)
    u_two, states = call(
        functools.partial(state_kernel, float(channels * peers)),
        [(IN_VMEM, array) for array in (squares, value_early, value_late, steps)],
        [(IN_VMEM, (length * ROWS, LANES), F32), (IN_VMEM, flat, F32)],
        [pltpu.VMEM((length, LANES), F32)],
    )
    received = lax.all_to_all(
        states.reshape(shares), "ctx", split_axis=0, concat_axis=0, tiled=True
    )
    conv_inner, decay = call(
        inner_kernel,
        [(IN_VMEM, array) for array in (u_two, steps, mode_weights, decay)],
        [(IN_VMEM, (length * ROWS, LANES), F32), (IN_VMEM, shares[1:], F32)],
    )
    (entries,) = call(
        scan_kernel, [(IN_VMEM, received), (IN_VMEM, decay)], [(IN_VMEM, shares, F32)]
    )
    entries = lax.all_to_all(entries, "ctx", split_axis=0, concat_axis=0, tiled=True)
    (mixed,) = call(
        output_kernel,
        [
            (IN_VMEM, array)
            for array in (entries.reshape(flat), conv_inner, steps, mode_weights, q_two)
        ],
        [(IN_HBM, (length, channels), BF16)],
        [
            pltpu.VMEM((length * ROWS, LANES), F32),
            pltpu.VMEM((length, channels), BF16),
            pltpu.SemaphoreType.DMA((QUARTERS,)),
        ],
    )
    return mixed


def solution(mesh):
    in_specs = (
        P("ctx", "tp"),
        P("ctx", "tp"),
        P("ctx", "tp"),
        P("tp", None),
        P("tp"),
        P("ctx", "tp"),
        P("ctx", "tp"),
        P(None, "tp"),
        P(None, "tp"),
    )
    return jax.shard_map(
        on_device, mesh=mesh, in_specs=in_specs, out_specs=P("ctx", "tp"), check_vma=False
    )
```
